32 devices in a mesh: slab: 8 (over z, y), mode: 4 (over x, core).
Axes of the slice: x: 2, y: 2, z: 4, core: 2. Of those that a mesh axis runs over, the one named last changes fastest.
Arguments:
- eigvec: bfloat16 [10240, 3, 1024], P('slab', None, 'mode'), may hold values from -6 to 6
- species: int32 [10240], P('slab'), may hold values from 0 to 3
- mode_cot: float32 [1024], P('mode'), may hold values from -4 to 4
- neighbours: int32 [10240, 16], P('slab'), may hold values from 0 to 2560, as said below
- pair_features: bfloat16 [163840, 128], P(('slab', 'mode')), may hold values from -130 to 130
- w_in: bfloat16 [128, 256], replicated, may hold values from -0.5 to 0.5
- b_in: float32 [256], replicated, may hold values from -3 to 3
- w_out: bfloat16 [9, 256], replicated, may hold values from -0.375 to 0.375
Outputs:
- features_grad: bfloat16 [163840, 128], P(('slab', 'mode'))
- grad_w_in: float32 [128, 256], replicated
- grad_b_in: float32 [256], replicated
- grad_w_out: float32 [9, 256], replicated
The draws below stay inside these ranges and needn't reach their ends.
Inputs may be any that keep to these rules, and one draw needn't show every extreme that they name: `neighbours`: atom r of a slab (0 to 1279) lists extended indices from r to r + 1280; extended index x stands for atom (slab * 1280 + x - 640) mod 10240; the value 1280 + 2 * 640 marks an empty slot.
All inputs are finite; a program needn't handle non-finite values.
Results may differ from the reference program's by a relative error of at most 0.019.
Values may be sent and summed in bfloat16 or wider, within the bound.
A program may use at most 64 MiB of HBM per device.

```python
import math
import jax
import jax.numpy as jnp
from jax import lax

A_DEV = 1280
RIM = 640
NBR = 16
MODES = 1024
F = 128
H = 256
ATOMS = 10240
PAIRS = 163840
N_SLAB = 8


def draw_neighbours(key, part):
    first_key, second_key = jax.random.split(key)
    local = jnp.arange(ATOMS, dtype=jnp.int32) % A_DEV
    slot = jnp.arange(NBR, dtype=jnp.int32)
    offset = jax.random.randint(first_key, (ATOMS, NBR), 0, 2 * RIM + 1)
    offset = jnp.where((local[:, None] == 0) & (slot[None, :] == 0), 0, offset)
    counts = jax.random.randint(second_key, (ATOMS,), 10, NBR + 1)
    counts = jnp.where(local == 0, 10, counts)
    live_slot = slot[None, :] < counts[:, None]
    return jnp.where(live_slot, local[:, None] + offset, A_DEV + 2 * RIM).astype(jnp.int32)


def draw_pair_features(key, part):
    col_key, base_key = jax.random.split(key, 2)
    column_scale = jnp.exp(jax.random.uniform(col_key, (F,), minval=0.0, maxval=math.log(10.0)))
    ramp = 1.0 + 2.0 * jnp.arange(PAIRS, dtype=jnp.float32) / PAIRS
    base = jnp.clip(jax.random.normal(base_key, (PAIRS, F)), -4.0, 4.0)
    return (base * ramp[:, None] * column_scale[None, :]).astype(jnp.bfloat16)


def with_ends(drawn, rng, low, high):
    longest = drawn.shape.index(max(drawn.shape))
    spots = []
    for shift in (0, 1):
        where = [jax.random.randint(jax.random.fold_in(rng, axis), (), 0, length) for axis, length in enumerate(drawn.shape)]
        where[longest] = (where[longest] + shift) % drawn.shape[longest]
        spots.append(tuple(where))
    return drawn.at[spots[0]].set(low).at[spots[1]].set(high)


def block_scale(own_key, shape, shards, low, high):
    gain = 1.0
    for position, parts in shards:
        heights = jax.random.uniform(jax.random.fold_in(jax.random.fold_in(own_key, 6), position), (parts,), jnp.float32, low / len(shards), high / len(shards))
        gain = gain * jnp.repeat(jnp.exp(heights), shape[position] // parts).reshape((-1,) + (1,) * (len(shape) - 1 - position))
    return gain


def centred(rng, dims, width, limit, shards=(), kind=jnp.bfloat16):
    values = width * jax.random.normal(rng, dims, jnp.float32)
    if shards:
        values = values * block_scale(rng, dims, shards, -0.22, 0.18)
    return jnp.clip(values, -limit, limit).astype(kind)


def setup_inputs(seed: int = 0) -> dict:
    keys = jax.random.split(jax.random.key(seed), 9)
    return {
        "eigvec": centred(keys[0], (ATOMS, 3, MODES), 1.0, 6.0, ((0, 8), (2, 4))),
        "species": with_ends(jax.random.randint(keys[1], (ATOMS,), 0, 4), jax.random.fold_in(keys[1], 1), 0, 3).astype(jnp.int32),
        "mode_cot": centred(keys[2], (MODES,), 1.0, 4.0, ((0, 4),), jnp.float32),
        "neighbours": draw_neighbours(jax.random.fold_in(keys[8], 71), 0),
        "pair_features": draw_pair_features(jax.random.fold_in(keys[8], 71), 0),
        "w_in": centred(keys[5], (F, H), F ** -0.5, 0.5),
        "b_in": centred(keys[6], (H,), 0.5, 3.0, (), jnp.float32),
        "w_out": centred(keys[7], (9, H), H ** -0.5, 0.375),
    }


MASS_TABLE = (1.35, 2.94, 2.79, 2.95)
CLIP_NORM = 100.0

def atom_masses(species):
    kinds = jnp.arange(4, dtype=jnp.int32)
    onehot = (species[:, None] == kinds[None, :]).astype(jnp.float32)
    return lax.optimization_barrier(jnp.sum(onehot * jnp.asarray(MASS_TABLE, jnp.float32)[None, :], axis=1))

def mlp_backward(features, pair_cot, w_in, b_in, w_out):
    preact = jnp.dot(features, w_in, preferred_element_type=jnp.float32) + b_in[None, :]
    sigmoid_pre = jax.nn.sigmoid(preact)
    hidden = (preact * sigmoid_pre).astype(jnp.bfloat16)
    hidden_cot = lax.dot_general(pair_cot, w_out, (((0,), (0,)), ((), ())), preferred_element_type=jnp.float32)
    pre_cot = (hidden_cot * sigmoid_pre * (1.0 + preact * (1.0 - sigmoid_pre))).astype(jnp.bfloat16)
    features_grad = lax.dot_general(pre_cot, w_in, (((1,), (1,)), ((), ())), preferred_element_type=jnp.float32).astype(jnp.bfloat16)
    grad_w_in = lax.dot_general(features, pre_cot, (((0,), (0,)), ((), ())), preferred_element_type=jnp.float32)
    grad_b_in = lax.optimization_barrier(jnp.sum(pre_cot.astype(jnp.float32), axis=0))
    grad_w_out = jnp.dot(pair_cot, hidden, preferred_element_type=jnp.float32)
    return (features_grad, grad_w_in, grad_b_in, grad_w_out)

def reference(eigvec, species, mode_cot, neighbours, pair_features, w_in, b_in, w_out):
    inv_root = lax.rsqrt(atom_masses(species))
    scaled = (eigvec.astype(jnp.float32) * inv_root[:, None, None]).astype(jnp.bfloat16)
    weighted = (scaled.astype(jnp.float32) * mode_cot[None, None, :]).astype(jnp.bfloat16)
    sentinel = A_DEV + 2 * RIM

    def per_slab(carry, slab_index):
        first_row = slab_index * A_DEV
        weighted_rows = lax.dynamic_slice_in_dim(weighted, first_row, A_DEV, 0).astype(jnp.float32)
        own_rows = lax.dynamic_slice_in_dim(scaled, first_row, A_DEV, 0).astype(jnp.float32)
        nbr_rows = lax.dynamic_slice_in_dim(neighbours, first_row, A_DEV, 0)
        live_mask = nbr_rows < sentinel
        partner_index = jnp.where(live_mask, (first_row + nbr_rows - RIM) % ATOMS, 0).astype(jnp.int32)
        partners = jnp.take(scaled, partner_index.reshape(-1), axis=0).reshape(A_DEV, NBR, 3, MODES).astype(jnp.float32)
        pair_terms = jnp.einsum('iam,ikbm->abik', weighted_rows, partners, precision=lax.Precision.HIGHEST).reshape(9, A_DEV, NBR)
        self_terms = jnp.einsum('iam,ibm->abi', weighted_rows, own_rows, precision=lax.Precision.HIGHEST).reshape(9, A_DEV)
        pair_cot = ((pair_terms - self_terms[:, :, None]) * live_mask[None].astype(jnp.float32)).astype(jnp.bfloat16)
        pair_cot = pair_cot.reshape(9, A_DEV * NBR)
        features = lax.dynamic_slice_in_dim(pair_features, first_row * NBR, A_DEV * NBR, 0)
        features_grad, part_w_in, part_b_in, part_w_out = mlp_backward(features, pair_cot, w_in, b_in, w_out)
        return ((carry[0] + part_w_in, carry[1] + part_b_in, carry[2] + part_w_out), features_grad)
    start = (jnp.zeros((F, H), jnp.float32), jnp.zeros((H,), jnp.float32), jnp.zeros((9, H), jnp.float32))
    sums, grads = lax.scan(per_slab, start, jnp.arange(N_SLAB, dtype=jnp.int32))
    raw_w_in, raw_b_in, raw_w_out = sums
    norm_sq = jnp.sum(raw_w_in * raw_w_in) + jnp.sum(raw_b_in * raw_b_in) + jnp.sum(raw_w_out * raw_w_out)
    factor = jnp.minimum(1.0, CLIP_NORM / jnp.sqrt(norm_sq + 1e-06))
    return (grads.reshape(PAIRS, F), raw_w_in * factor, raw_b_in * factor, raw_w_out * factor)
```

```python
import functools

import jax
import jax.numpy as jnp
import numpy as np
from jax import lax
from jax.experimental import pallas as pl
from jax.experimental.pallas import tpu as pltpu
from jax.sharding import PartitionSpec as P

MASS_TABLE = (1.35, 2.94, 2.79, 2.95)
CLIP_NORM = 100.0
TILE = 128
VMEM_LIMIT = 60 * 1024 * 1024
MESH = pl.DeviceIdType.MESH
VMEM = pl.BlockSpec(memory_space=pltpu.VMEM)
SMEM = pl.BlockSpec(memory_space=pltpu.SMEM)


def inverse_root_mass(species):
    kinds = jnp.arange(4, dtype=jnp.int32)
    onehot = (species[:, None] == kinds[None, :]).astype(jnp.float32)
    masses = jnp.sum(onehot * jnp.asarray(MASS_TABLE, jnp.float32)[None, :], axis=1)
    return lax.rsqrt(masses)


def task_table(tasks):
    tasks = list(tasks)
    while len(tasks) % 2:
        tasks.append((tasks[-1][0], tasks[-1][1], -1))
    tasks.append((tasks[-1][0], tasks[-1][1], -1))
    return np.asarray(tasks, np.int32).T.copy()


def rows_of(block):
    return pl.ds(pl.multiple_of(block * TILE, TILE), TILE)


def band_tasks(table, own_ref, partner_ref, cot_ref, low_ref, high_ref, total_ref, even_ref, odd_ref):
    count = table.shape[1] - 1

    def product(task, dest):
        block, partner = table[0, task], table[1, task]
        cot = cot_ref[...]
        left = jnp.concatenate(
            [(own_ref[a, rows_of(block), :].astype(jnp.float32) * cot).astype(jnp.bfloat16) for a in range(3)], axis=0
        )
        right = jnp.concatenate([partner_ref[b, rows_of(partner), :] for b in range(3)], axis=0)
        dest[...] = lax.dot_general(left, right, (((1,), (1,)), ((), ())), preferred_element_type=jnp.float32)

    def select(task, source):
        block, distance = table[0, task], table[2, task]
        first = pl.multiple_of(block * TILE, TILE)
        for group in range(TILE // 8):
            rows = pl.ds(first + 8 * group, 8)
            lane = low_ref[rows, :]
            hit = high_ref[rows, :] == distance
            for a in range(3):
                for b in range(3):
                    values = source[a * TILE + 8 * group : a * TILE + 8 * group + 8, b * TILE : (b + 1) * TILE]
                    picked = jnp.take_along_axis(values, lane, axis=1, mode="promise_in_bounds")
                    total_ref[3 * a + b, rows, :] = jnp.where(hit, picked, total_ref[3 * a + b, rows, :])

    product(0, even_ref)

    def step(pair, _):
        product(2 * pair + 1, odd_ref)
        select(2 * pair, even_ref)
        product(2 * pair + 2, even_ref)
        select(2 * pair + 1, odd_ref)
        return 0

    lax.fori_loop(0, count // 2, step, 0)


def slot_tables(nbr_ref, low_ref, high_ref, block):
    slots = nbr_ref[:, rows_of(block)]
    spread = jnp.transpose(jnp.concatenate([slots] * (TILE // slots.shape[0]), axis=0))
    offset = spread - block * TILE
    low_ref[rows_of(block), :] = offset & (TILE - 1)
    high_ref[rows_of(block), :] = lax.shift_right_arithmetic(offset, 7)
    return spread


def packed(total_ref, block, slot_count):
    lanes = lax.broadcasted_iota(jnp.int32, (TILE, TILE), 1)
    position = lanes // slot_count
    first = jnp.zeros((TILE, TILE), jnp.float32)
    for part in range(8):
        first = jnp.where(position == part, total_ref[part, rows_of(block), :], first)
    last = jnp.where(position == 0, total_ref[8, rows_of(block), :], 0.0)
    return first, last


def own_kernel(table, own_ref, cot_ref, nbr_ref, out_ref, low_ref, high_ref, total_ref, even_ref, odd_ref):
    atom_count = own_ref.shape[1]
    slot_count = nbr_ref.shape[0]
    blocks = atom_count // TILE
    sentinel = 2 * atom_count

    def begin(block, _):
        slot_tables(nbr_ref, low_ref, high_ref, block)
        cot = cot_ref[...]
        own = [own_ref[b, rows_of(block), :].astype(jnp.float32) for b in range(3)]
        for a in range(3):
            left = (own[a] * cot).astype(jnp.bfloat16).astype(jnp.float32)
            for b in range(3):
                same = jnp.sum(left * own[b], axis=1, keepdims=True)
                total_ref[3 * a + b, rows_of(block), :] = jnp.zeros((TILE, TILE), jnp.float32)
                total_ref[9 + 3 * a + b, rows_of(block), :] = jnp.broadcast_to(same, (TILE, TILE))
        return 0

    lax.fori_loop(0, blocks, begin, 0)
    band_tasks(table, own_ref, own_ref, cot_ref, low_ref, high_ref, total_ref, even_ref, odd_ref)

    def finish(block, _):
        live = (high_ref[rows_of(block), :] * TILE + low_ref[rows_of(block), :] + block * TILE) < sentinel
        first, last = packed(total_ref, block, slot_count)
        self_first, self_last = packed(total_ref.at[9:18], block, slot_count)
        out_ref[rows_of(block), 0:TILE] = jnp.where(live, first - self_first, 0.0)
        out_ref[rows_of(block), TILE : 2 * TILE] = jnp.where(live, last - self_last, 0.0)
        return 0

    lax.fori_loop(0, blocks, finish, 0)


def rim_kernel(low_table, high_table, own_ref, low_rim, high_rim, cot_ref, nbr_ref, part_ref, out_ref,
               low_ref, high_ref, total_ref, even_ref, odd_ref):
    atom_count = own_ref.shape[1]
    slot_count = nbr_ref.shape[0]
    blocks = atom_count // TILE

    def begin(block, _):
        slot_tables(nbr_ref, low_ref, high_ref, block)
        for part in range(9):
            total_ref[part, rows_of(block), :] = jnp.zeros((TILE, TILE), jnp.float32)
        return 0

    lax.fori_loop(0, blocks, begin, 0)
    band_tasks(low_table, own_ref, low_rim, cot_ref, low_ref, high_ref, total_ref, even_ref, odd_ref)
    band_tasks(high_table, own_ref, high_rim, cot_ref, low_ref, high_ref, total_ref, even_ref, odd_ref)

    def finish(block, _):
        first, last = packed(total_ref, block, slot_count)
        rows = rows_of(block)
        out_ref[rows, 0:TILE] = (part_ref[rows, 0:TILE] + first).astype(jnp.bfloat16)
        out_ref[rows, TILE : 2 * TILE] = (part_ref[rows, TILE : 2 * TILE] + last).astype(jnp.bfloat16)
        return 0

    lax.fori_loop(0, blocks, finish, 0)


def scatter_kernel(groups, in_ref, out_ref, held, send_sem, recv_sem):
    slab = lax.axis_index("slab")
    me = lax.axis_index("mode")
    barrier = pltpu.get_barrier_semaphore()
    for hop in range(1, groups):
        pl.semaphore_signal(barrier, inc=1, device_id=(slab, lax.rem(me + hop, groups)), device_id_type=MESH)
    pl.semaphore_wait(barrier, groups - 1)
    copies = []
    for hop in range(1, groups):
        peer = lax.rem(me + hop, groups)
        copies.append(pltpu.make_async_remote_copy(
            src_ref=in_ref.at[peer], dst_ref=held.at[hop - 1], send_sem=send_sem.at[hop - 1],
            recv_sem=recv_sem.at[hop - 1], device_id=(slab, peer), device_id_type=MESH))
    for copy in copies:
        copy.start()
    total = in_ref[me].astype(jnp.float32)
    for copy in copies:
        copy.wait()
    for hop in range(1, groups):
        total = total + held[hop - 1].astype(jnp.float32)
    out_ref[...] = total


def mlp_kernel(slot_count, x_ref, cot_ref, w_in_ref, b_in_ref, w_rep_ref, grad_ref, sums_ref, w_out_sum):
    rows = min(512, x_ref.shape[0])
    atoms = rows // slot_count
    features = x_ref.shape[1]
    hidden_width = w_in_ref.shape[1]
    width = cot_ref.shape[1]
    sums_ref[...] = jnp.zeros_like(sums_ref)
    w_out_sum[...] = jnp.zeros_like(w_out_sum)
    row = lax.broadcasted_iota(jnp.int32, (rows, width), 0)
    lane = lax.broadcasted_iota(jnp.int32, (rows, width), 1)
    keep = lax.rem(row, slot_count) == lax.rem(lane, slot_count)

    def step(index, _):
        here = pl.ds(pl.multiple_of(index * rows, rows), rows)
        x = x_ref[here, :]
        preact = jnp.dot(x, w_in_ref[...], preferred_element_type=jnp.float32) + b_in_ref[...]
        gate = jax.nn.sigmoid(preact)
        hidden = (preact * gate).astype(jnp.bfloat16)
        block = cot_ref[pl.ds(pl.multiple_of(index * atoms, atoms), atoms), :]
        spread = jnp.broadcast_to(block[:, None, :], (atoms, slot_count, width)).reshape(rows, width)
        spread = jnp.where(keep, spread, 0.0).astype(jnp.bfloat16)
        hidden_cot = jnp.dot(spread, w_rep_ref[...], preferred_element_type=jnp.float32)
        pre_cot = (hidden_cot * gate * (1.0 + preact * (1.0 - gate))).astype(jnp.bfloat16)
        grad_ref[here, :] = lax.dot_general(
            pre_cot, w_in_ref[...], (((1,), (1,)), ((), ())), preferred_element_type=jnp.float32
        ).astype(jnp.bfloat16)
        sums_ref[0:features, :] += lax.dot_general(
            x, pre_cot, (((0,), (0,)), ((), ())), preferred_element_type=jnp.float32)
        sums_ref[features : features + 1, :] += jnp.sum(pre_cot.astype(jnp.float32), axis=0, keepdims=True)
        w_out_sum[...] += lax.dot_general(
            spread, hidden, (((0,), (0,)), ((), ())), preferred_element_type=jnp.float32)
        return 0

    lax.fori_loop(0, x_ref.shape[0] // rows, step, 0)
    for part in range(9):
        sums_ref[features + 1 + part : features + 2 + part, :] = jnp.sum(
            w_out_sum[part * slot_count : (part + 1) * slot_count, :], axis=0, keepdims=True)


def total_kernel(slabs, groups, features, in_ref, w_in_out, b_in_out, w_out_out,
                 held, mine, everyone, send_sem, recv_sem, back_send, back_recv):
    count = slabs * groups
    owners = in_ref.shape[0]
    me = lax.axis_index("slab") * groups + lax.axis_index("mode")

    def device(index):
        return (index // groups, lax.rem(index, groups))

    barrier = pltpu.get_barrier_semaphore()

    def greet(hop, _):
        pl.semaphore_signal(barrier, inc=1, device_id=device(lax.rem(me + hop, count)), device_id_type=MESH)
        return 0

    lax.fori_loop(1, count, greet, 0)
    pl.semaphore_wait(barrier, count - 1)

    def to_owner(owner):
        return pltpu.make_async_remote_copy(
            src_ref=in_ref.at[owner], dst_ref=held.at[me], send_sem=send_sem.at[owner],
            recv_sem=recv_sem.at[me], device_id=device(owner), device_id_type=MESH)

    def from_source(source):
        return pltpu.make_async_remote_copy(
            src_ref=in_ref.at[0], dst_ref=held.at[source], send_sem=send_sem.at[0],
            recv_sem=recv_sem.at[source], device_id=device(source), device_id_type=MESH)

    def to_all(target):
        return pltpu.make_async_remote_copy(
            src_ref=mine, dst_ref=everyone.at[me], send_sem=back_send.at[target],
            recv_sem=back_recv.at[me], device_id=device(target), device_id_type=MESH)

    def from_owner(owner):
        return pltpu.make_async_remote_copy(
            src_ref=mine, dst_ref=everyone.at[owner], send_sem=back_send.at[0],
            recv_sem=back_recv.at[owner], device_id=device(owner), device_id_type=MESH)

    def others(length, act):
        def body(index, _):
            @pl.when(index != me)
            def _():
                act(index)
            return 0
        lax.fori_loop(0, length, body, 0)

    others(owners, lambda owner: to_owner(owner).start())

    @pl.when(me < owners)
    def _():
        others(count, lambda source: from_source(source).wait_recv())
        mine[...] = in_ref[me]

        def add(source):
            mine[...] += held[source]

        others(count, add)
        others(count, lambda target: to_all(target).start())
        everyone[me] = mine[...]

    others(owners, lambda owner: to_owner(owner).wait_send())
    others(owners, lambda owner: from_owner(owner).wait_recv())

    @pl.when(me < owners)
    def _():
        others(count, lambda target: to_all(target).wait_send())

    raw = everyone[...].reshape(owners * 8, everyone.shape[2])
    factor = jnp.minimum(1.0, CLIP_NORM / jnp.sqrt(jnp.sum(raw * raw, keepdims=True) + 1e-6))
    scaled = raw * factor
    w_in_out[...] = scaled[0:features, :]
    b_in_out[...] = scaled[features : features + 1, :]
    w_out_out[...] = scaled[features + 1 : features + 10, :]


def shards(slabs, groups, eigvec, species, mode_cot, neighbours, pair_features, w_in, b_in, w_out):
    atoms, _, modes = eigvec.shape
    slot_count = neighbours.shape[1]
    rim = atoms // 2
    blocks, rim_blocks = atoms // TILE, rim // TILE
    features, hidden_width = w_in.shape

    inv_root = inverse_root_mass(species)
    panel = jnp.transpose(eigvec, (1, 0, 2))
    scaled = (panel.astype(jnp.float32) * inv_root[None, :, None]).astype(jnp.bfloat16)
    forward = [(i, (i + 1) % slabs) for i in range(slabs)]
    backward = [(target, source) for source, target in forward]
    low_rim = lax.ppermute(scaled[:, atoms - rim :, :], "slab", forward)
    high_rim = lax.ppermute(scaled[:, :rim, :], "slab", backward)
    nbr = neighbours.T
    cot = mode_cot[None, :]

    reach = 2 * rim_blocks
    own_tasks, low_tasks, high_tasks = [], [], []
    for block in range(blocks):
        for distance in range(reach + 1):
            partner = block + distance - rim_blocks
            if partner < 0:
                low_tasks.append((block, partner + rim_blocks, distance))
            elif partner < blocks:
                own_tasks.append((block, partner, distance))
            else:
                high_tasks.append((block, partner - blocks, distance))
    own_table, low_table, high_table = task_table(own_tasks), task_table(low_tasks), task_table(high_tasks)

    def band_scratch(parts):
        return [
            pltpu.VMEM((atoms, TILE), jnp.int32),
            pltpu.VMEM((atoms, TILE), jnp.int32),
            pltpu.VMEM((parts, atoms, TILE), jnp.float32),
            pltpu.VMEM((3 * TILE, 3 * TILE), jnp.float32),
            pltpu.VMEM((3 * TILE, 3 * TILE), jnp.float32),
        ]

    params = pltpu.CompilerParams(vmem_limit_bytes=VMEM_LIMIT)
    own_part = pl.pallas_call(
        own_kernel,
        out_shape=jax.ShapeDtypeStruct((atoms, 2 * TILE), jnp.float32),
        in_specs=[SMEM, VMEM, VMEM, VMEM],
        out_specs=VMEM,
        scratch_shapes=band_scratch(18),
        compiler_params=params,
        name="own_pairs",
    )(own_table, scaled, cot, nbr)
    pair_part = pl.pallas_call(
        rim_kernel,
        out_shape=jax.ShapeDtypeStruct((atoms, 2 * TILE), jnp.bfloat16),
        in_specs=[SMEM, SMEM] + [VMEM] * 6,
        out_specs=VMEM,
        scratch_shapes=band_scratch(9),
        compiler_params=params,
        name="rim_pairs",
    )(low_table, high_table, scaled, low_rim, high_rim, cot, nbr, own_part)

    share = atoms // groups
    pair_cot = pl.pallas_call(
        functools.partial(scatter_kernel, groups),
        out_shape=jax.ShapeDtypeStruct((share, 2 * TILE), jnp.float32),
        in_specs=[VMEM],
        out_specs=VMEM,
        scratch_shapes=[
            pltpu.VMEM((groups - 1, share, 2 * TILE), jnp.bfloat16),
            pltpu.SemaphoreType.DMA((groups - 1,)),
            pltpu.SemaphoreType.DMA((groups - 1,)),
        ],
        compiler_params=pltpu.CompilerParams(collective_id=0, has_side_effects=True),
        name="mode_scatter",
    )(pair_part.reshape(groups, share, 2 * TILE))

    w_rep = jnp.pad(jnp.repeat(w_out, slot_count, axis=0), ((0, 2 * TILE - 9 * slot_count), (0, 0)))
    owners = -(-(features + 10) // 8)
    features_grad, sums = pl.pallas_call(
        functools.partial(mlp_kernel, slot_count),
        out_shape=(
            jax.ShapeDtypeStruct(pair_features.shape, jnp.bfloat16),
            jax.ShapeDtypeStruct((owners * 8, hidden_width), jnp.float32),
        ),
        in_specs=[VMEM] * 5,
        out_specs=(VMEM, VMEM),
        scratch_shapes=[pltpu.VMEM((2 * TILE, hidden_width), jnp.float32)],
        compiler_params=params,
        name="pair_network",
    )(pair_features, pair_cot, w_in, b_in[None, :], w_rep)

    count = slabs * groups
    grad_w_in, grad_b_in, grad_w_out = pl.pallas_call(
        functools.partial(total_kernel, slabs, groups, features),
        out_shape=(
            jax.ShapeDtypeStruct((features, hidden_width), jnp.float32),
            jax.ShapeDtypeStruct((1, hidden_width), jnp.float32),
            jax.ShapeDtypeStruct((9, hidden_width), jnp.float32),
        ),
        in_specs=[VMEM],
        out_specs=(VMEM, VMEM, VMEM),
        scratch_shapes=[
            pltpu.VMEM((count, 8, hidden_width), jnp.float32),
            pltpu.VMEM((8, hidden_width), jnp.float32),
            pltpu.VMEM((owners, 8, hidden_width), jnp.float32),
            pltpu.SemaphoreType.DMA((owners,)),
            pltpu.SemaphoreType.DMA((count,)),
            pltpu.SemaphoreType.DMA((count,)),
            pltpu.SemaphoreType.DMA((owners,)),
        ],
        compiler_params=pltpu.CompilerParams(collective_id=1, has_side_effects=True),
        name="gradient_total",
    )(sums.reshape(owners, 8, hidden_width))
    return features_grad, grad_w_in, grad_b_in.reshape(hidden_width), grad_w_out


def solution(mesh):
    return jax.shard_map(
        functools.partial(shards, mesh.shape["slab"], mesh.shape["mode"]),
        mesh=mesh,
        in_specs=(
            P("slab", None, "mode"),
            P("slab"),
            P("mode"),
            P("slab", None),
            P(("slab", "mode"), None),
            P(),
            P(),
            P(),
        ),
        out_specs=(P(("slab", "mode"), None), P(), P(), P()),
        check_vma=False,
    )
```

```python
import functools

import jax
import jax.numpy as jnp
import numpy as np
from jax import lax
from jax.experimental import pallas as pl
from jax.experimental.pallas import tpu as pltpu
from jax.sharding import PartitionSpec as P

MASS_TABLE = (1.35, 2.94, 2.79, 2.95)
CLIP_NORM = 100.0
TILE = 128
VMEM_LIMIT = 60 * 1024 * 1024
MESH = pl.DeviceIdType.MESH
VMEM = pl.BlockSpec(memory_space=pltpu.VMEM)
SMEM = pl.BlockSpec(memory_space=pltpu.SMEM)


def inverse_root_mass(species):
    kinds = jnp.arange(4, dtype=jnp.int32)
    onehot = (species[:, None] == kinds[None, :]).astype(jnp.float32)
    masses = jnp.sum(onehot * jnp.asarray(MASS_TABLE, jnp.float32)[None, :], axis=1)
    return lax.rsqrt(masses)


def task_table(tasks):
    tasks = list(tasks)
    while len(tasks) % 2:
        tasks.append((tasks[-1][0], tasks[-1][1], -1))
    tasks.append((tasks[-1][0], tasks[-1][1], -1))
    return np.asarray(tasks, np.int32).T.copy()


def rows_of(block):
    return pl.ds(pl.multiple_of(block * TILE, TILE), TILE)


def band_tasks(table, own_ref, partner_ref, cot_ref, low_ref, high_ref, total_ref, even_ref, odd_ref):
    count = table.shape[1] - 1

    def product(task, dest):
        block, partner = table[0, task], table[1, task]
        cot = cot_ref[...]
        left = jnp.concatenate(
            [(own_ref[a, rows_of(block), :].astype(jnp.float32) * cot).astype(jnp.bfloat16) for a in range(3)], axis=0
        )
        right = jnp.concatenate([partner_ref[b, rows_of(partner), :] for b in range(3)], axis=0)
        dest[...] = lax.dot_general(left, right, (((1,), (1,)), ((), ())), preferred_element_type=jnp.float32)

    def select(task, source):
        block, distance = table[0, task], table[2, task]
        first = pl.multiple_of(block * TILE, TILE)
        for group in range(TILE // 8):
            rows = pl.ds(first + 8 * group, 8)
            lane = low_ref[rows, :]
            hit = high_ref[rows, :] == distance
            for a in range(3):
                for b in range(3):
                    values = source[a * TILE + 8 * group : a * TILE + 8 * group + 8, b * TILE : (b + 1) * TILE]
                    picked = jnp.take_along_axis(values, lane, axis=1, mode="promise_in_bounds")
                    total_ref[3 * a + b, rows, :] = jnp.where(hit, picked, total_ref[3 * a + b, rows, :])

    product(0, even_ref)

    def step(pair, _):
        product(2 * pair + 1, odd_ref)
        select(2 * pair, even_ref)
        product(2 * pair + 2, even_ref)
        select(2 * pair + 1, odd_ref)
        return 0

    lax.fori_loop(0, count // 2, step, 0)


def slot_tables(nbr_ref, low_ref, high_ref, block):
    slots = nbr_ref[:, rows_of(block)]
    spread = jnp.transpose(jnp.concatenate([slots] * (TILE // slots.shape[0]), axis=0))
    offset = spread - block * TILE
    low_ref[rows_of(block), :] = offset & (TILE - 1)
    high_ref[rows_of(block), :] = lax.shift_right_arithmetic(offset, 7)
    return spread


def packed(total_ref, block, slot_count):
    lanes = lax.broadcasted_iota(jnp.int32, (TILE, TILE), 1)
    position = lanes // slot_count
    first = jnp.zeros((TILE, TILE), jnp.float32)
    for part in range(8):
        first = jnp.where(position == part, total_ref[part, rows_of(block), :], first)
    return first, total_ref[8, rows_of(block), :]


def own_kernel(table, own_ref, cot_ref, nbr_ref, out_ref, low_ref, high_ref, total_ref, even_ref, odd_ref):
    atom_count = own_ref.shape[1]
    slot_count = nbr_ref.shape[0]
    blocks = atom_count // TILE
    sentinel = 2 * atom_count

    def begin(block, _):
        slot_tables(nbr_ref, low_ref, high_ref, block)
        cot = cot_ref[...]
        own = [own_ref[b, rows_of(block), :].astype(jnp.float32) for b in range(3)]
        for a in range(3):
            left = (own[a] * cot).astype(jnp.bfloat16).astype(jnp.float32)
            for b in range(3):
                same = jnp.sum(left * own[b], axis=1, keepdims=True)
                total_ref[3 * a + b, rows_of(block), :] = jnp.zeros((TILE, TILE), jnp.float32)
                total_ref[9 + 3 * a + b, rows_of(block), :] = jnp.broadcast_to(same, (TILE, TILE))
        return 0

    lax.fori_loop(0, blocks, begin, 0)
    band_tasks(table, own_ref, own_ref, cot_ref, low_ref, high_ref, total_ref, even_ref, odd_ref)

    def finish(block, _):
        live = (high_ref[rows_of(block), :] * TILE + low_ref[rows_of(block), :] + block * TILE) < sentinel
        first, last = packed(total_ref, block, slot_count)
        self_first, self_last = packed(total_ref.at[9:18], block, slot_count)
        out_ref[rows_of(block), 0:TILE] = jnp.where(live, first - self_first, 0.0)
        out_ref[rows_of(block), TILE : 2 * TILE] = jnp.where(live, last - self_last, 0.0)
        return 0

    lax.fori_loop(0, blocks, finish, 0)


def rim_kernel(touched, final, low_table, high_table, own_ref, low_rim, high_rim, cot_ref, nbr_ref, part_ref,
               out_ref, low_ref, high_ref, total_ref, even_ref, odd_ref, fold_ref):
    atom_count = own_ref.shape[1]
    slot_count = nbr_ref.shape[0]
    blocks = atom_count // TILE

    for block in touched:
        slot_tables(nbr_ref, low_ref, high_ref, block)
        for part in range(9):
            total_ref[part, rows_of(block), :] = jnp.zeros((TILE, TILE), jnp.float32)
    band_tasks(low_table, own_ref, low_rim, cot_ref, low_ref, high_ref, total_ref, even_ref, odd_ref)
    band_tasks(high_table, own_ref, high_rim, cot_ref, low_ref, high_ref, total_ref, even_ref, odd_ref)

    fold = 8 * TILE // slot_count
    position = lax.broadcasted_iota(jnp.int32, (8, TILE), 1) // slot_count
    for block in range(blocks):
        rows = pl.ds(block * TILE, TILE)
        first, last = part_ref[rows, 0:TILE], part_ref[rows, TILE : 2 * TILE]
        if block in touched:
            more_first, more_last = packed(total_ref, block, slot_count)
            first, last = first + more_first, last + more_last
        if not final:
            out_ref[rows, 0:TILE] = first
            out_ref[rows, TILE : 2 * TILE] = last
            continue
        share = out_ref.shape[1] * fold // (fold + 8)
        for unit in range(TILE // fold):
            atom = block * TILE + unit * fold
            group, row = atom // share, atom % share
            out_ref[group, row : row + fold, :] = first[unit * fold : (unit + 1) * fold].astype(jnp.bfloat16)
            folded = jnp.zeros((8, TILE), jnp.float32)
            for p in range(fold // 8):
                start = unit * fold + 8 * p
                folded = jnp.where(position == p, last[start : start + 8], folded)
            fold_ref[group, row // fold * 8 : row // fold * 8 + 8, :] = folded
    if final:
        out_ref[:, share:, :] = fold_ref[...].astype(jnp.bfloat16)


def scatter_kernel(groups, in_ref, out_ref, held, send_sem, recv_sem):
    slab = lax.axis_index("slab")
    me = lax.axis_index("mode")
    barrier = pltpu.get_barrier_semaphore()
    for hop in range(1, groups):
        pl.semaphore_signal(barrier, inc=1, device_id=(slab, lax.rem(me + hop, groups)), device_id_type=MESH)
    pl.semaphore_wait(barrier, groups - 1)
    copies = []
    for hop in range(1, groups):
        peer = lax.rem(me + hop, groups)
        copies.append(pltpu.make_async_remote_copy(
            src_ref=in_ref.at[peer], dst_ref=held.at[hop - 1], send_sem=send_sem.at[hop - 1],
            recv_sem=recv_sem.at[hop - 1], device_id=(slab, peer), device_id_type=MESH))
    for copy in copies:
        copy.start()
    total = in_ref[me].astype(jnp.float32)
    for copy in copies:
        copy.wait()
    for hop in range(1, groups):
        total = total + held[hop - 1].astype(jnp.float32)
    out_ref[...] = total


def mlp_kernel(slot_count, x_ref, cot_ref, w_in_ref, b_in_ref, w_rep_ref, grad_ref, sums_ref, w_out_sum):
    share = x_ref.shape[0] // slot_count
    fold = 8 * TILE // slot_count
    atoms = fold
    rows = atoms * slot_count
    features = x_ref.shape[1]
    sums_ref[...] = jnp.zeros_like(sums_ref)
    w_out_sum[...] = jnp.zeros_like(w_out_sum)
    row = lax.broadcasted_iota(jnp.int32, (rows, TILE), 0)
    lane = lax.broadcasted_iota(jnp.int32, (rows, TILE), 1)
    keep = lax.rem(row, slot_count) == lax.rem(lane, slot_count)
    keep_last = keep & (row // (8 * slot_count) == lane // slot_count)

    def expand(block, mask):
        wide = jnp.broadcast_to(block[:, None, :], (atoms, slot_count, TILE)).reshape(rows, TILE)
        return jnp.where(mask, wide, 0.0).astype(jnp.bfloat16)

    def step(index, _):
        here = pl.ds(pl.multiple_of(index * rows, rows), rows)
        x = x_ref[here, :]
        preact = jnp.dot(x, w_in_ref[...], preferred_element_type=jnp.float32) + b_in_ref[...]
        gate = jax.nn.sigmoid(preact)
        hidden = (preact * gate).astype(jnp.bfloat16)
        first = cot_ref[pl.ds(pl.multiple_of(index * atoms, atoms), atoms), :]
        last = cot_ref[pl.ds(pl.multiple_of(share + index * 8, 8), 8), :]
        spread = jnp.concatenate(
            [expand(first, keep), expand(jnp.concatenate([last] * (atoms // 8), axis=0), keep_last)], axis=1)
        hidden_cot = jnp.dot(spread, w_rep_ref[...], preferred_element_type=jnp.float32)
        pre_cot = (hidden_cot * gate * (1.0 + preact * (1.0 - gate))).astype(jnp.bfloat16)
        grad_ref[here, :] = lax.dot_general(
            pre_cot, w_in_ref[...], (((1,), (1,)), ((), ())), preferred_element_type=jnp.float32
        ).astype(jnp.bfloat16)
        sums_ref[0:features, :] += lax.dot_general(
            x, pre_cot, (((0,), (0,)), ((), ())), preferred_element_type=jnp.float32)
        sums_ref[features : features + 1, :] += jnp.sum(pre_cot.astype(jnp.float32), axis=0, keepdims=True)
        w_out_sum[...] += lax.dot_general(
            spread, hidden, (((0,), (0,)), ((), ())), preferred_element_type=jnp.float32)
        return 0

    lax.fori_loop(0, x_ref.shape[0] // rows, step, 0)
    for part in range(9):
        end = (part + 1) * slot_count if part < 8 else 2 * TILE
        sums_ref[features + 1 + part : features + 2 + part, :] = jnp.sum(
            w_out_sum[part * slot_count : end, :], axis=0, keepdims=True)


def total_kernel(slabs, groups, in_ref, everyone, held, mine, rounds, summed, near_send, near_recv, far_send, far_recv, back_send, back_recv):
    slab, mode = lax.axis_index("slab"), lax.axis_index("mode")
    barrier = pltpu.get_barrier_semaphore()

    def peer_mode(hop):
        return lax.rem(mode + hop, groups)

    def peer_slab(hop):
        return lax.rem(slab + hop, slabs)

    for hop in range(1, groups):
        pl.semaphore_signal(barrier, inc=1, device_id=(slab, peer_mode(hop)), device_id_type=MESH)

    def greet(hop, _):
        pl.semaphore_signal(barrier, inc=1, device_id=(peer_slab(hop), mode), device_id_type=MESH)
        return 0

    lax.fori_loop(1, slabs, greet, 0)
    pl.semaphore_wait(barrier, groups - 1 + slabs - 1)

    near = [pltpu.make_async_remote_copy(
        src_ref=in_ref.at[peer_mode(hop)], dst_ref=held.at[hop - 1], send_sem=near_send.at[hop - 1],
        recv_sem=near_recv.at[hop - 1], device_id=(slab, peer_mode(hop)), device_id_type=MESH)
        for hop in range(1, groups)]
    for copy in near:
        copy.start()
    total = in_ref[mode]
    for copy in near:
        copy.wait()
    for hop in range(1, groups):
        total = total + held[hop - 1]
    mine[...] = total.astype(jnp.bfloat16)

    def far(hop):
        return pltpu.make_async_remote_copy(
            src_ref=mine, dst_ref=rounds.at[slab], send_sem=far_send.at[hop],
            recv_sem=far_recv.at[slab], device_id=(peer_slab(hop), mode), device_id_type=MESH)

    def far_from(hop):
        return pltpu.make_async_remote_copy(
            src_ref=mine, dst_ref=rounds.at[peer_slab(hop)], send_sem=far_send.at[hop],
            recv_sem=far_recv.at[peer_slab(hop)], device_id=(peer_slab(hop), mode), device_id_type=MESH)

    def send(hop, _):
        far(hop).start()
        return 0

    def settle(hop, _):
        far_from(hop).wait_recv()
        return 0

    def sent(hop, _):
        far(hop).wait_send()
        return 0

    lax.fori_loop(1, slabs, send, 0)
    rounds[slab] = mine[...]
    lax.fori_loop(1, slabs, settle, 0)
    summed[...] = lax.fori_loop(
        1, slabs, lambda index, value: value + rounds[index].astype(jnp.float32), rounds[0].astype(jnp.float32))

    back = [pltpu.make_async_remote_copy(
        src_ref=summed, dst_ref=everyone.at[mode], send_sem=back_send.at[hop - 1],
        recv_sem=back_recv.at[hop - 1], device_id=(slab, peer_mode(hop)), device_id_type=MESH)
        for hop in range(1, groups)]
    for copy in back:
        copy.start()
    everyone[mode] = summed[...]
    lax.fori_loop(1, slabs, sent, 0)
    for copy in back:
        copy.wait()


def clip_kernel(raw_ref, w_in_out, b_in_out, w_out_out):
    features = w_in_out.shape[0]
    raw = raw_ref[...]
    factor = jnp.minimum(1.0, CLIP_NORM / jnp.sqrt(jnp.sum(raw * raw, keepdims=True) + 1e-6))
    scaled = raw * factor
    w_in_out[...] = scaled[0:features, :]
    b_in_out[...] = scaled[features : features + 1, :].reshape(b_in_out.shape)
    w_out_out[...] = scaled[features + 1 : features + 10, :]


def shards(slabs, groups, eigvec, species, mode_cot, neighbours, pair_features, w_in, b_in, w_out):
    atoms, _, modes = eigvec.shape
    slot_count = neighbours.shape[1]
    rim = atoms // 2
    blocks, rim_blocks = atoms // TILE, rim // TILE
    features, hidden_width = w_in.shape

    inv_root = inverse_root_mass(species)
    panel = jnp.transpose(eigvec, (1, 0, 2))
    scaled = (panel.astype(jnp.float32) * inv_root[None, :, None]).astype(jnp.bfloat16)
    forward = [(i, (i + 1) % slabs) for i in range(slabs)]
    backward = [(target, source) for source, target in forward]
    far_blocks = max(1, 2 * rim_blocks // 5)
    far = far_blocks * TILE
    near_low = lax.ppermute(scaled[:, atoms - rim + far :, :], "slab", forward)
    near_high = lax.ppermute(scaled[:, : rim - far, :], "slab", backward)
    far_low = lax.ppermute(scaled[:, atoms - rim : atoms - rim + far, :], "slab", forward)
    far_high = lax.ppermute(scaled[:, rim - far : rim, :], "slab", backward)
    nbr = neighbours.T
    cot = mode_cot[None, :]

    reach = 2 * rim_blocks
    near_blocks = rim_blocks - far_blocks
    own_tasks, near_low_tasks, near_high_tasks, far_low_tasks, far_high_tasks = [], [], [], [], []
    for block in range(blocks):
        for distance in range(reach + 1):
            partner = block + distance - rim_blocks
            if partner < -near_blocks:
                far_low_tasks.append((block, partner + rim_blocks, distance))
            elif partner < 0:
                near_low_tasks.append((block, partner + near_blocks, distance))
            elif partner < blocks:
                own_tasks.append((block, partner, distance))
            elif partner < blocks + near_blocks:
                near_high_tasks.append((block, partner - blocks, distance))
            else:
                far_high_tasks.append((block, partner - blocks - near_blocks, distance))
    share = atoms // groups
    fold = 8 * TILE // slot_count
    share_rows = share + share * 8 // fold

    def band_scratch(parts):
        return [
            pltpu.VMEM((atoms, TILE), jnp.int32),
            pltpu.VMEM((atoms, TILE), jnp.int32),
            pltpu.VMEM((parts, atoms, TILE), jnp.float32),
            pltpu.VMEM((3 * TILE, 3 * TILE), jnp.float32),
            pltpu.VMEM((3 * TILE, 3 * TILE), jnp.float32),
        ]

    def rim_pairs(low_tasks, high_tasks, low_rim, high_rim, part, final):
        touched = tuple(sorted({task[0] for task in low_tasks + high_tasks}))
        shape = (groups, share_rows, TILE) if final else (atoms, 2 * TILE)
        return pl.pallas_call(
            functools.partial(rim_kernel, touched, final),
            out_shape=jax.ShapeDtypeStruct(shape, jnp.bfloat16 if final else jnp.float32),
            in_specs=[SMEM, SMEM] + [VMEM] * 6,
            out_specs=VMEM,
            scratch_shapes=band_scratch(9) + [pltpu.VMEM((groups, share_rows - share, TILE), jnp.float32)],
            compiler_params=params,
            name="far_pairs" if final else "near_pairs",
        )(task_table(low_tasks), task_table(high_tasks), scaled, low_rim, high_rim, cot, nbr, part)

    params = pltpu.CompilerParams(vmem_limit_bytes=VMEM_LIMIT)
    own_part = pl.pallas_call(
        own_kernel,
        out_shape=jax.ShapeDtypeStruct((atoms, 2 * TILE), jnp.float32),
        in_specs=[SMEM, VMEM, VMEM, VMEM],
        out_specs=VMEM,
        scratch_shapes=band_scratch(18),
        compiler_params=params,
        name="own_pairs",
    )(task_table(own_tasks), scaled, cot, nbr)
    near_part = rim_pairs(near_low_tasks, near_high_tasks, near_low, near_high, own_part, False)
    pair_part = rim_pairs(far_low_tasks, far_high_tasks, far_low, far_high, near_part, True)
    pair_cot = pl.pallas_call(
        functools.partial(scatter_kernel, groups),
        out_shape=jax.ShapeDtypeStruct((share_rows, TILE), jnp.float32),
        in_specs=[VMEM],
        out_specs=VMEM,
        scratch_shapes=[
            pltpu.VMEM((groups - 1, share_rows, TILE), jnp.bfloat16),
            pltpu.SemaphoreType.DMA((groups - 1,)),
            pltpu.SemaphoreType.DMA((groups - 1,)),
        ],
        compiler_params=pltpu.CompilerParams(collective_id=0, has_side_effects=True),
        name="mode_scatter",
    )(pair_part)

    parts = TILE // slot_count
    w_rep = jnp.concatenate([
        jnp.broadcast_to(w_out[:parts, None, :], (parts, slot_count, hidden_width)).reshape(TILE, hidden_width),
        jnp.broadcast_to(w_out[parts:], (TILE, hidden_width))])
    quarter = -(-(features + 10) // (groups * 8)) * 8
    features_grad, sums = pl.pallas_call(
        functools.partial(mlp_kernel, slot_count),
        out_shape=(
            jax.ShapeDtypeStruct(pair_features.shape, jnp.bfloat16),
            jax.ShapeDtypeStruct((groups * quarter, hidden_width), jnp.float32),
        ),
        in_specs=[VMEM] * 5,
        out_specs=(VMEM, VMEM),
        scratch_shapes=[pltpu.VMEM((2 * TILE, hidden_width), jnp.float32)],
        compiler_params=params,
        name="pair_network",
    )(pair_features, pair_cot, w_in, b_in[None, :], w_rep)

    raw = pl.pallas_call(
        functools.partial(total_kernel, slabs, groups),
        out_shape=jax.ShapeDtypeStruct((groups, quarter, hidden_width), jnp.float32),
        in_specs=[VMEM],
        out_specs=VMEM,
        scratch_shapes=[
            pltpu.VMEM((groups - 1, quarter, hidden_width), jnp.float32),
            pltpu.VMEM((quarter, hidden_width), jnp.bfloat16),
            pltpu.VMEM((slabs, quarter, hidden_width), jnp.bfloat16),
            pltpu.VMEM((quarter, hidden_width), jnp.float32),
            pltpu.SemaphoreType.DMA((groups - 1,)),
            pltpu.SemaphoreType.DMA((groups - 1,)),
            pltpu.SemaphoreType.DMA((slabs,)),
            pltpu.SemaphoreType.DMA((slabs,)),
            pltpu.SemaphoreType.DMA((groups - 1,)),
            pltpu.SemaphoreType.DMA((groups - 1,)),
        ],
        compiler_params=pltpu.CompilerParams(collective_id=1, has_side_effects=True),
        name="gradient_total",
    )(sums.reshape(groups, quarter, hidden_width))
    grad_w_in, grad_b_in, grad_w_out = pl.pallas_call(
        clip_kernel,
        out_shape=(
            jax.ShapeDtypeStruct((features, hidden_width), jnp.float32),
            jax.ShapeDtypeStruct((hidden_width,), jnp.float32),
            jax.ShapeDtypeStruct((9, hidden_width), jnp.float32),
        ),
        in_specs=[VMEM],
        out_specs=(VMEM, VMEM, VMEM),
        compiler_params=params,
        name="clip",
    )(raw.reshape(groups * quarter, hidden_width))
    return features_grad, grad_w_in, grad_b_in, grad_w_out


def solution(mesh):
    return jax.shard_map(
        functools.partial(shards, mesh.shape["slab"], mesh.shape["mode"]),
        mesh=mesh,
        in_specs=(
            P("slab", None, "mode"),
            P("slab"),
            P("mode"),
            P("slab", None),
            P(("slab", "mode"), None),
            P(),
            P(),
            P(),
        ),
        out_specs=(P(("slab", "mode"), None), P(), P(), P()),
        check_vma=False,
    )
```

```python
import functools

import jax
import jax.numpy as jnp
import numpy as np
from jax import lax
from jax.experimental import pallas as pl
from jax.experimental.pallas import tpu as pltpu
from jax.sharding import PartitionSpec as P

MASS_TABLE = (1.35, 2.94, 2.79, 2.95)
CLIP_NORM = 100.0
TILE = 128
VMEM_LIMIT = 28 * 1024 * 1024
MESH = pl.DeviceIdType.MESH
VMEM = pl.BlockSpec(memory_space=pltpu.VMEM)
SMEM = pl.BlockSpec(memory_space=pltpu.SMEM)


def inverse_root_mass(species):
    kinds = jnp.arange(4, dtype=jnp.int32)
    onehot = (species[:, None] == kinds[None, :]).astype(jnp.float32)
    masses = jnp.sum(onehot * jnp.asarray(MASS_TABLE, jnp.float32)[None, :], axis=1)
    return lax.rsqrt(masses)


def task_table(tasks):
    tasks = list(tasks)
    while len(tasks) % 2:
        tasks.append((tasks[-1][0], tasks[-1][1], -1))
    tasks.append((tasks[-1][0], tasks[-1][1], -1))
    return np.asarray(tasks, np.int32).T.copy()


def rows_of(block):
    return pl.ds(pl.multiple_of(block * TILE, TILE), TILE)


def band_tasks(table, own_ref, partner_ref, cot_ref, low_ref, high_ref, total_ref, even_ref, odd_ref):
    count = table.shape[1] - 1

    def product(task, dest):
        block, partner = table[0, task], table[1, task]
        cot = cot_ref[...]
        left = jnp.concatenate(
            [(own_ref[a, rows_of(block), :].astype(jnp.float32) * cot).astype(jnp.bfloat16) for a in range(3)], axis=0
        )
        right = jnp.concatenate([partner_ref[b, rows_of(partner), :] for b in range(3)], axis=0)
        dest[...] = lax.dot_general(left, right, (((1,), (1,)), ((), ())), preferred_element_type=jnp.float32)

    def select(task, source):
        block, distance = table[0, task], table[2, task]
        first = pl.multiple_of(block * TILE, TILE)
        for group in range(TILE // 8):
            rows = pl.ds(first + 8 * group, 8)
            lane = low_ref[rows, :]
            hit = high_ref[rows, :] == distance
            for a in range(3):
                for b in range(3):
                    values = source[a * TILE + 8 * group : a * TILE + 8 * group + 8, b * TILE : (b + 1) * TILE]
                    picked = jnp.take_along_axis(values, lane, axis=1, mode="promise_in_bounds")
                    total_ref[3 * a + b, rows, :] = jnp.where(hit, picked, total_ref[3 * a + b, rows, :])

    product(0, even_ref)

    def step(pair, _):
        product(2 * pair + 1, odd_ref)
        select(2 * pair, even_ref)
        product(2 * pair + 2, even_ref)
        select(2 * pair + 1, odd_ref)
        return 0

    lax.fori_loop(0, count // 2, step, 0)


def slot_tables(nbr_ref, low_ref, high_ref, block):
    slots = nbr_ref[:, rows_of(block)]
    spread = jnp.transpose(jnp.concatenate([slots] * (TILE // slots.shape[0]), axis=0))
    offset = spread - block * TILE
    low_ref[rows_of(block), :] = offset & (TILE - 1)
    high_ref[rows_of(block), :] = lax.shift_right_arithmetic(offset, 7)
    return spread


def packed(total_ref, block, slot_count):
    lanes = lax.broadcasted_iota(jnp.int32, (TILE, TILE), 1)
    position = lanes // slot_count
    first = jnp.zeros((TILE, TILE), jnp.float32)
    for part in range(8):
        first = jnp.where(position == part, total_ref[part, rows_of(block), :], first)
    return first, total_ref[8, rows_of(block), :]


def own_kernel(table, own_ref, cot_ref, nbr_ref, out_ref, low_ref, high_ref, total_ref, even_ref, odd_ref):
    atom_count = own_ref.shape[1]
    slot_count = nbr_ref.shape[0]
    blocks = atom_count // TILE
    sentinel = 2 * atom_count

    def begin(block, _):
        slot_tables(nbr_ref, low_ref, high_ref, block)
        cot = cot_ref[...]
        own = [own_ref[b, rows_of(block), :].astype(jnp.float32) for b in range(3)]
        for a in range(3):
            left = (own[a] * cot).astype(jnp.bfloat16).astype(jnp.float32)
            for b in range(3):
                same = jnp.sum(left * own[b], axis=1, keepdims=True)
                total_ref[3 * a + b, rows_of(block), :] = jnp.zeros((TILE, TILE), jnp.float32)
                total_ref[9 + 3 * a + b, rows_of(block), :] = jnp.broadcast_to(same, (TILE, TILE))
        return 0

    lax.fori_loop(0, blocks, begin, 0)
    band_tasks(table, own_ref, own_ref, cot_ref, low_ref, high_ref, total_ref, even_ref, odd_ref)

    def finish(block, _):
        live = (high_ref[rows_of(block), :] * TILE + low_ref[rows_of(block), :] + block * TILE) < sentinel
        first, last = packed(total_ref, block, slot_count)
        self_first, self_last = packed(total_ref.at[9:18], block, slot_count)
        out_ref[rows_of(block), 0:TILE] = jnp.where(live, first - self_first, 0.0)
        out_ref[rows_of(block), TILE : 2 * TILE] = jnp.where(live, last - self_last, 0.0)
        return 0

    lax.fori_loop(0, blocks, finish, 0)


def rim_kernel(touched, final, low_table, high_table, own_ref, low_rim, high_rim, cot_ref, nbr_ref, part_ref,
               out_ref, low_ref, high_ref, total_ref, even_ref, odd_ref, fold_ref):
    atom_count = own_ref.shape[1]
    slot_count = nbr_ref.shape[0]
    blocks = atom_count // TILE

    for block in touched:
        slot_tables(nbr_ref, low_ref, high_ref, block)
        for part in range(9):
            total_ref[part, rows_of(block), :] = jnp.zeros((TILE, TILE), jnp.float32)
    band_tasks(low_table, own_ref, low_rim, cot_ref, low_ref, high_ref, total_ref, even_ref, odd_ref)
    band_tasks(high_table, own_ref, high_rim, cot_ref, low_ref, high_ref, total_ref, even_ref, odd_ref)

    fold = 8 * TILE // slot_count
    position = lax.broadcasted_iota(jnp.int32, (8, TILE), 1) // slot_count
    for block in range(blocks):
        rows = pl.ds(block * TILE, TILE)
        first, last = part_ref[rows, 0:TILE], part_ref[rows, TILE : 2 * TILE]
        if block in touched:
            more_first, more_last = packed(total_ref, block, slot_count)
            first, last = first + more_first, last + more_last
        if not final:
            out_ref[rows, 0:TILE] = first
            out_ref[rows, TILE : 2 * TILE] = last
            continue
        share = out_ref.shape[1] * fold // (fold + 8)
        for unit in range(TILE // fold):
            atom = block * TILE + unit * fold
            group, row = atom // share, atom % share
            out_ref[group, row : row + fold, :] = first[unit * fold : (unit + 1) * fold].astype(jnp.bfloat16)
            folded = jnp.zeros((8, TILE), jnp.float32)
            for p in range(fold // 8):
                start = unit * fold + 8 * p
                folded = jnp.where(position == p, last[start : start + 8], folded)
            fold_ref[group, row // fold * 8 : row // fold * 8 + 8, :] = folded
    if final:
        out_ref[:, share:, :] = fold_ref[...].astype(jnp.bfloat16)


def scatter_kernel(groups, in_ref, out_ref, held, send_sem, recv_sem):
    slab = lax.axis_index("slab")
    me = lax.axis_index("mode")
    barrier = pltpu.get_barrier_semaphore()
    for hop in range(1, groups):
        pl.semaphore_signal(barrier, inc=1, device_id=(slab, lax.rem(me + hop, groups)), device_id_type=MESH)
    pl.semaphore_wait(barrier, groups - 1)
    copies = []
    for hop in range(1, groups):
        peer = lax.rem(me + hop, groups)
        copies.append(pltpu.make_async_remote_copy(
            src_ref=in_ref.at[peer], dst_ref=held.at[hop - 1], send_sem=send_sem.at[hop - 1],
            recv_sem=recv_sem.at[hop - 1], device_id=(slab, peer), device_id_type=MESH))
    for copy in copies:
        copy.start()
    total = in_ref[me].astype(jnp.float32)
    for copy in copies:
        copy.wait()
    for hop in range(1, groups):
        total = total + held[hop - 1].astype(jnp.float32)
    out_ref[...] = total


def mlp_kernel(slot_count, x_ref, cot_ref, w_in_ref, b_in_ref, w_rep_ref, grad_ref, sums_ref, w_out_sum):
    share = x_ref.shape[0] // slot_count
    fold = 8 * TILE // slot_count
    atoms = fold
    rows = atoms * slot_count
    features = x_ref.shape[1]
    sums_ref[...] = jnp.zeros_like(sums_ref)
    w_out_sum[...] = jnp.zeros_like(w_out_sum)
    row = lax.broadcasted_iota(jnp.int32, (rows, TILE), 0)
    lane = lax.broadcasted_iota(jnp.int32, (rows, TILE), 1)
    keep = lax.rem(row, slot_count) == lax.rem(lane, slot_count)
    keep_last = keep & (row // (8 * slot_count) == lane // slot_count)

    def expand(block, mask):
        wide = jnp.broadcast_to(block[:, None, :], (atoms, slot_count, TILE)).reshape(rows, TILE)
        return jnp.where(mask, wide, 0.0).astype(jnp.bfloat16)

    def step(index, _):
        here = pl.ds(pl.multiple_of(index * rows, rows), rows)
        x = x_ref[here, :]
        preact = jnp.dot(x, w_in_ref[...], preferred_element_type=jnp.float32) + b_in_ref[...]
        gate = jax.nn.sigmoid(preact)
        hidden = (preact * gate).astype(jnp.bfloat16)
        first = cot_ref[pl.ds(pl.multiple_of(index * atoms, atoms), atoms), :]
        last = cot_ref[pl.ds(pl.multiple_of(share + index * 8, 8), 8), :]
        spread = jnp.concatenate(
            [expand(first, keep), expand(jnp.concatenate([last] * (atoms // 8), axis=0), keep_last)], axis=1)
        hidden_cot = jnp.dot(spread, w_rep_ref[...], preferred_element_type=jnp.float32)
        pre_cot = (hidden_cot * gate * (1.0 + preact * (1.0 - gate))).astype(jnp.bfloat16)
        grad_ref[here, :] = lax.dot_general(
            pre_cot, w_in_ref[...], (((1,), (1,)), ((), ())), preferred_element_type=jnp.float32
        ).astype(jnp.bfloat16)
        sums_ref[0:features, :] += lax.dot_general(
            x, pre_cot, (((0,), (0,)), ((), ())), preferred_element_type=jnp.float32)
        sums_ref[features : features + 1, :] += jnp.sum(pre_cot.astype(jnp.float32), axis=0, keepdims=True)
        w_out_sum[...] += lax.dot_general(
            spread, hidden, (((0,), (0,)), ((), ())), preferred_element_type=jnp.float32)
        return 0

    lax.fori_loop(0, x_ref.shape[0] // rows, step, 0)
    for part in range(9):
        end = (part + 1) * slot_count if part < 8 else 2 * TILE
        sums_ref[features + 1 + part : features + 2 + part, :] = jnp.sum(
            w_out_sum[part * slot_count : end, :], axis=0, keepdims=True)


def total_kernel(slabs, groups, in_ref, everyone, held, mine, rounds, summed, near_send, near_recv, far_send, far_recv, back_send, back_recv):
    slab, mode = lax.axis_index("slab"), lax.axis_index("mode")
    barrier = pltpu.get_barrier_semaphore()

    def peer_mode(hop):
        return lax.rem(mode + hop, groups)

    def peer_slab(hop):
        return lax.rem(slab + hop, slabs)

    for hop in range(1, groups):
        pl.semaphore_signal(barrier, inc=1, device_id=(slab, peer_mode(hop)), device_id_type=MESH)

    def greet(hop, _):
        pl.semaphore_signal(barrier, inc=1, device_id=(peer_slab(hop), mode), device_id_type=MESH)
        return 0

    lax.fori_loop(1, slabs, greet, 0)
    pl.semaphore_wait(barrier, groups - 1 + slabs - 1)

    near = [pltpu.make_async_remote_copy(
        src_ref=in_ref.at[peer_mode(hop)], dst_ref=held.at[hop - 1], send_sem=near_send.at[hop - 1],
        recv_sem=near_recv.at[hop - 1], device_id=(slab, peer_mode(hop)), device_id_type=MESH)
        for hop in range(1, groups)]
    for copy in near:
        copy.start()
    total = in_ref[mode]
    for copy in near:
        copy.wait()
    for hop in range(1, groups):
        total = total + held[hop - 1]
    mine[...] = total.astype(jnp.bfloat16)

    def far(hop):
        return pltpu.make_async_remote_copy(
            src_ref=mine, dst_ref=rounds.at[slab], send_sem=far_send.at[hop],
            recv_sem=far_recv.at[slab], device_id=(peer_slab(hop), mode), device_id_type=MESH)

    def far_from(hop):
        return pltpu.make_async_remote_copy(
            src_ref=mine, dst_ref=rounds.at[peer_slab(hop)], send_sem=far_send.at[hop],
            recv_sem=far_recv.at[peer_slab(hop)], device_id=(peer_slab(hop), mode), device_id_type=MESH)

    def send(hop, _):
        far(hop).start()
        return 0

    def settle(hop, _):
        far_from(hop).wait_recv()
        return 0

    def sent(hop, _):
        far(hop).wait_send()
        return 0

    lax.fori_loop(1, slabs, send, 0)
    rounds[slab] = mine[...]
    lax.fori_loop(1, slabs, settle, 0)
    summed[...] = lax.fori_loop(
        1, slabs, lambda index, value: value + rounds[index].astype(jnp.float32), rounds[0].astype(jnp.float32))

    back = [pltpu.make_async_remote_copy(
        src_ref=summed, dst_ref=everyone.at[mode], send_sem=back_send.at[hop - 1],
        recv_sem=back_recv.at[hop - 1], device_id=(slab, peer_mode(hop)), device_id_type=MESH)
        for hop in range(1, groups)]
    for copy in back:
        copy.start()
    everyone[mode] = summed[...]
    lax.fori_loop(1, slabs, sent, 0)
    for copy in back:
        copy.wait()


def clip_kernel(raw_ref, w_in_out, b_in_out, w_out_out):
    features = w_in_out.shape[0]
    raw = raw_ref[...]
    factor = jnp.minimum(1.0, CLIP_NORM / jnp.sqrt(jnp.sum(raw * raw, keepdims=True) + 1e-6))
    scaled = raw * factor
    w_in_out[...] = scaled[0:features, :]
    b_in_out[...] = scaled[features : features + 1, :].reshape(b_in_out.shape)
    w_out_out[...] = scaled[features + 1 : features + 10, :]


def shards(slabs, groups, eigvec, species, mode_cot, neighbours, pair_features, w_in, b_in, w_out):
    atoms, _, modes = eigvec.shape
    slot_count = neighbours.shape[1]
    rim = atoms // 2
    blocks, rim_blocks = atoms // TILE, rim // TILE
    features, hidden_width = w_in.shape

    inv_root = inverse_root_mass(species)
    panel = jnp.transpose(eigvec, (1, 0, 2))
    scaled = (panel.astype(jnp.float32) * inv_root[None, :, None]).astype(jnp.bfloat16)
    forward = [(i, (i + 1) % slabs) for i in range(slabs)]
    backward = [(target, source) for source, target in forward]
    far_blocks = max(1, 2 * rim_blocks // 5)
    far = far_blocks * TILE
    near_low = lax.ppermute(scaled[:, atoms - rim + far :, :], "slab", forward)
    near_high = lax.ppermute(scaled[:, : rim - far, :], "slab", backward)
    far_low = lax.ppermute(scaled[:, atoms - rim : atoms - rim + far, :], "slab", forward)
    far_high = lax.ppermute(scaled[:, rim - far : rim, :], "slab", backward)
    nbr = neighbours.T
    cot = mode_cot[None, :]

    reach = 2 * rim_blocks
    near_blocks = rim_blocks - far_blocks
    own_tasks, near_low_tasks, near_high_tasks, far_low_tasks, far_high_tasks = [], [], [], [], []
    for block in range(blocks):
        for distance in range(reach + 1):
            partner = block + distance - rim_blocks
            if partner < -near_blocks:
                far_low_tasks.append((block, partner + rim_blocks, distance))
            elif partner < 0:
                near_low_tasks.append((block, partner + near_blocks, distance))
            elif partner < blocks:
                own_tasks.append((block, partner, distance))
            elif partner < blocks + near_blocks:
                near_high_tasks.append((block, partner - blocks, distance))
            else:
                far_high_tasks.append((block, partner - blocks - near_blocks, distance))
    share = atoms // groups
    fold = 8 * TILE // slot_count
    share_rows = share + share * 8 // fold

    def band_scratch(parts):
        return [
            pltpu.VMEM((atoms, TILE), jnp.int32),
            pltpu.VMEM((atoms, TILE), jnp.int32),
            pltpu.VMEM((parts, atoms, TILE), jnp.float32),
            pltpu.VMEM((3 * TILE, 3 * TILE), jnp.float32),
            pltpu.VMEM((3 * TILE, 3 * TILE), jnp.float32),
        ]

    def rim_pairs(low_tasks, high_tasks, low_rim, high_rim, part, final):
        touched = tuple(sorted({task[0] for task in low_tasks + high_tasks}))
        shape = (groups, share_rows, TILE) if final else (atoms, 2 * TILE)
        return pl.pallas_call(
            functools.partial(rim_kernel, touched, final),
            out_shape=jax.ShapeDtypeStruct(shape, jnp.bfloat16 if final else jnp.float32),
            in_specs=[SMEM, SMEM] + [VMEM] * 6,
            out_specs=VMEM,
            scratch_shapes=band_scratch(9) + [pltpu.VMEM((groups, share_rows - share, TILE), jnp.float32)],
            compiler_params=params,
            name="far_pairs" if final else "near_pairs",
        )(task_table(low_tasks), task_table(high_tasks), scaled, low_rim, high_rim, cot, nbr, part)

    params = pltpu.CompilerParams(vmem_limit_bytes=VMEM_LIMIT)
    own_part = pl.pallas_call(
        own_kernel,
        out_shape=jax.ShapeDtypeStruct((atoms, 2 * TILE), jnp.float32),
        in_specs=[SMEM, VMEM, VMEM, VMEM],
        out_specs=VMEM,
        scratch_shapes=band_scratch(18),
        compiler_params=params,
        name="own_pairs",
    )(task_table(own_tasks), scaled, cot, nbr)
    near_part = rim_pairs(near_low_tasks, near_high_tasks, near_low, near_high, own_part, False)
    pair_part = rim_pairs(far_low_tasks, far_high_tasks, far_low, far_high, near_part, True)
    pair_cot = pl.pallas_call(
        functools.partial(scatter_kernel, groups),
        out_shape=jax.ShapeDtypeStruct((share_rows, TILE), jnp.float32),
        in_specs=[VMEM],
        out_specs=VMEM,
        scratch_shapes=[
            pltpu.VMEM((groups - 1, share_rows, TILE), jnp.bfloat16),
            pltpu.SemaphoreType.DMA((groups - 1,)),
            pltpu.SemaphoreType.DMA((groups - 1,)),
        ],
        compiler_params=pltpu.CompilerParams(collective_id=0, has_side_effects=True),
        name="mode_scatter",
    )(pair_part)

    parts = TILE // slot_count
    w_rep = jnp.concatenate([
        jnp.broadcast_to(w_out[:parts, None, :], (parts, slot_count, hidden_width)).reshape(TILE, hidden_width),
        jnp.broadcast_to(w_out[parts:], (TILE, hidden_width))])
    quarter = -(-(features + 10) // (groups * 8)) * 8
    features_grad, sums = pl.pallas_call(
        functools.partial(mlp_kernel, slot_count),
        out_shape=(
            jax.ShapeDtypeStruct(pair_features.shape, jnp.bfloat16),
            jax.ShapeDtypeStruct((groups * quarter, hidden_width), jnp.float32),
        ),
        in_specs=[VMEM] * 5,
        out_specs=(VMEM, VMEM),
        scratch_shapes=[pltpu.VMEM((2 * TILE, hidden_width), jnp.float32)],
        compiler_params=params,
        name="pair_network",
    )(pair_features, pair_cot, w_in, b_in[None, :], w_rep)

    raw = pl.pallas_call(
        functools.partial(total_kernel, slabs, groups),
        out_shape=jax.ShapeDtypeStruct((groups, quarter, hidden_width), jnp.float32),
        in_specs=[VMEM],
        out_specs=VMEM,
        scratch_shapes=[
            pltpu.VMEM((groups - 1, quarter, hidden_width), jnp.float32),
            pltpu.VMEM((quarter, hidden_width), jnp.bfloat16),
            pltpu.VMEM((slabs, quarter, hidden_width), jnp.bfloat16),
            pltpu.VMEM((quarter, hidden_width), jnp.float32),
            pltpu.SemaphoreType.DMA((groups - 1,)),
            pltpu.SemaphoreType.DMA((groups - 1,)),
            pltpu.SemaphoreType.DMA((slabs,)),
            pltpu.SemaphoreType.DMA((slabs,)),
            pltpu.SemaphoreType.DMA((groups - 1,)),
            pltpu.SemaphoreType.DMA((groups - 1,)),
        ],
        compiler_params=pltpu.CompilerParams(collective_id=1, has_side_effects=True),
        name="gradient_total",
    )(sums.reshape(groups, quarter, hidden_width))
    grad_w_in, grad_b_in, grad_w_out = pl.pallas_call(
        clip_kernel,
        out_shape=(
            jax.ShapeDtypeStruct((features, hidden_width), jnp.float32),
            jax.ShapeDtypeStruct((hidden_width,), jnp.float32),
            jax.ShapeDtypeStruct((9, hidden_width), jnp.float32),
        ),
        in_specs=[VMEM],
        out_specs=(VMEM, VMEM, VMEM),
        compiler_params=params,
        name="clip",
    )(raw.reshape(groups * quarter, hidden_width))
    return features_grad, grad_w_in, grad_b_in, grad_w_out


def solution(mesh):
    return jax.shard_map(
        functools.partial(shards, mesh.shape["slab"], mesh.shape["mode"]),
        mesh=mesh,
        in_specs=(
            P("slab", None, "mode"),
            P("slab"),
            P("mode"),
            P("slab", None),
            P(("slab", "mode"), None),
            P(),
            P(),
            P(),
        ),
        out_specs=(P(("slab", "mode"), None), P(), P(), P()),
        check_vma=False,
    )
```
